512 devices in a mesh: mp: 8 (over z), section: 4 (over x_hi, core), dp: 16 (over y, x_lo).
Axes of the slice: x: 4 (x_hi: 2, x_lo: 2; x = x_hi * 2 + x_lo), y: 8, z: 8, core: 2. Of those that a mesh axis runs over, the one named last changes fastest.
Arguments:
- residual_in: float32 [4, 5120, 1024], P('section', ('dp', 'mp')), parts along dimension 1
- pre_activation: bfloat16 [4, 5120, 8192], P('section', 'dp', 'mp'), parts along dimension 1, may hold values from -6 to 6
- down_projection: bfloat16 [4, 8192, 1024], P('section', 'mp'), may hold values from -0.0625 to 0.0625
- attention_gain: float32 [4, 1024], P('section'), may hold values from 0.1 to 1.9
- qkv_projection: bfloat16 [4, 1024, 16, 384], P('section', None, 'mp'), may hold values from -0.1875 to 0.1875
- layer_counts: int32 [4], P('section'), may hold values from 1 to 8
Outputs:
- finished_stream: float32 [4, 5120, 1024], P('section', ('dp', 'mp')), parts along dimension 1
- qkv_heads: bfloat16 [4, 5120, 16, 384], P('section', 'dp', 'mp'), parts along dimension 1
The draws below stay inside these ranges and needn't reach their ends.
There are 16 independent parts, one for each index of `dp`. The reference program is written for one: setup_inputs(seed, part) draws one part's arguments, and reference() takes and returns one part's arrays. A program takes and returns all parts, laid end to end along the dimension named above; an argument that names none is the same for every part. Nothing has to cross between parts.
All inputs are finite; a program needn't handle non-finite values.
Results may differ from the reference program's by a relative error of at most 0.001.
The reference program's roundings to bfloat16 on the way (of `hidden` and `normed`) count: a program that leaves them out, or rounds other values in their place, can miss the bound.
Values may be sent and summed in bfloat16 or wider, within the bound.
A program may use at most 64 MiB of HBM per device.

```python
import jax
import jax.numpy as jnp
from jax import lax

D = 1024
FFW = 8192
HEADS = 16
DK = 128
MAXCOUNT = 8
ROWS = 320
SECTIONS = 4


def draw_residual_in(key, part):
    key_base = jax.random.fold_in(key, 11)
    normal_part = jnp.clip(jax.random.normal(key_base, (SECTIONS, ROWS, D), jnp.float32), -6.0, 6.0)
    return normal_part


def plant(entries, rng, least, top_value):
    shape = entries.shape
    spot = [jax.random.randint(jax.random.fold_in(rng, axis), (), 0, shape[axis]) for axis in range(len(shape))]
    entries = entries.at[tuple(spot)].set(least)
    longest = shape.index(max(shape))
    spot[longest] = (spot[longest] + 1) % shape[longest]
    return entries.at[tuple(spot)].set(top_value)


def level_of(own_key, extent, pieces, smallest, largest):
    def one(dim, parts):
        steps = jax.random.uniform(jax.random.fold_in(jax.random.fold_in(own_key, 6), dim), (parts,), jnp.float32, smallest / len(pieces), largest / len(pieces))
        return jnp.repeat(jnp.exp(steps), extent[dim] // parts).reshape((-1,) + (1,) * (len(extent) - dim - 1))

    level = one(*pieces[0])
    for cut in pieces[1:]:
        level = level * one(*cut)
    return level


def gaussian(rng, extent, scale, reach, shards=(), kind=jnp.bfloat16):
    drawn = jax.random.normal(rng, extent, jnp.float32) * scale
    if len(shards) > 0:
        drawn = level_of(rng, extent, shards, -0.22, 0.18) * drawn
    return jnp.clip(drawn, min=-reach, max=reach).astype(kind)


def setup_inputs(seed: int = 0, part: int = 0) -> dict:
    streams_of = jax.random.split(jax.random.key(seed), 7)
    own_keys = jax.random.split(jax.random.fold_in(streams_of[6], part), 7)
    return {
        "residual_in": draw_residual_in(jax.random.fold_in(jax.random.fold_in(streams_of[6], part), 71), part),
        "pre_activation": gaussian(own_keys[1], (SECTIONS, ROWS, FFW), 1.0, 6.0, ((0, 4), (2, 8))),
        "down_projection": gaussian(streams_of[2], (SECTIONS, FFW, D), FFW ** -0.5, 0.0625, ((0, 4), (1, 8))),
        "attention_gain": jnp.clip(1.0 + 0.18 * jax.random.normal(streams_of[3], (SECTIONS, D), jnp.float32), 0.1, 1.9),
        "qkv_projection": gaussian(streams_of[4], (SECTIONS, D, HEADS, 3 * DK), D ** -0.5, 0.1875, ((0, 4), (2, 8))),
        "layer_counts": plant(jax.random.randint(streams_of[5], (SECTIONS,), 1, MAXCOUNT + 1), jax.random.fold_in(streams_of[5], 1), 1, MAXCOUNT).astype(jnp.int32),
    }


def reference(residual_in, pre_activation, down_projection, attention_gain, qkv_projection, layer_counts):
    depth_total = jnp.sum(layer_counts).astype(jnp.int32)
    branch_scale = 1.0 / jnp.sqrt(depth_total.astype(jnp.float32))
    finished = []
    for number in range(SECTIONS):
        hidden = jnp.maximum(pre_activation[number], jnp.zeros((), pre_activation.dtype))
        branch = jnp.dot(hidden, down_projection[number], preferred_element_type=jnp.float32)
        finished.append(residual_in[number] + branch * branch_scale)
    outputs = []
    for number in range(SECTIONS):
        incoming = finished[(number - 1) % SECTIONS]
        mean_square = lax.optimization_barrier(jnp.mean(incoming * incoming, axis=-1, keepdims=True))
        normed = (incoming * lax.rsqrt(mean_square + 1e-06) * attention_gain[number]).astype(jnp.bfloat16)
        qkv_matrix = qkv_projection[number].reshape(D, HEADS * 3 * DK)
        product = jnp.dot(normed, qkv_matrix, preferred_element_type=jnp.float32).astype(jnp.bfloat16)
        outputs.append(product.reshape(ROWS, HEADS, 3 * DK))
    return (jnp.stack(finished), jnp.stack(outputs))
```

```python
import functools

import jax
import jax.numpy as jnp
from jax import lax
from jax.experimental import pallas as pl
from jax.experimental.pallas import tpu as pltpu
from jax.sharding import PartitionSpec as P

MESH = pl.DeviceIdType.MESH
GROUP = 8


def event_order(ring, groups):
    half = ring // 2
    step, gap, hop, relay = 2.9, 0.7, 3.0, 1.9
    events = []
    for g in range(groups):
        for k in range(1, half):
            events.append((k * step + g * gap, ("sum", k, g)))
        done = half * step + g * gap
        events.append((done, ("finish", half, g)))
        for h in range(1, half + 1):
            events.append((done + hop + (h - 1) * relay, ("pass", h, g)))
    events.sort()
    return [event for _, event in events]


def kernel(
    ring, sections,
    residual_ref, pre_ref, down_ref, gain_ref, qkv_ref, counts_ref,
    finished_ref, out_ref,
    hidden, down, qkv, residual, next_gain, counts, partial, arrived, normed, rows_all,
    load_sem, small_send, small_recv, sum_send, sum_recv, hop_send, hop_recv, pass_send, pass_recv,
):
    me = lax.axis_index("mp")
    sec = lax.axis_index("section")
    half = ring // 2
    rows, width = residual.shape[0], residual.shape[1]
    groups = rows // GROUP
    cut = width // 2
    up, below = lax.rem(me + 1, ring), lax.rem(me + ring - 1, ring)
    after, before = lax.rem(sec + 1, sections), lax.rem(sec + sections - 1, sections)

    order = [half]
    for away in range(half - 1, 0, -1):
        order += [away, ring - away]
    order.append(0)
    loads = {}

    def load(name, src, dst, slot):
        loads[name] = pltpu.make_async_copy(src, dst, load_sem.at[slot])
        loads[name].start()

    def load_rows(r):
        start = pl.multiple_of(lax.rem(me + r, ring) * rows, 8)
        load(r, pre_ref.at[0, pl.ds(start, rows), :], hidden.at[r], r)

    load_rows(order[0])
    load("down", down_ref.at[0], down, ring)
    for r in order[1:]:
        load_rows(r)
    load("residual", residual_ref.at[0], residual, ring + 1)
    load("qkv", qkv_ref, qkv, ring + 2)

    counts[0] = jnp.full(counts.shape[1:], counts_ref[0], jnp.int32)

    barrier = pltpu.get_barrier_semaphore()
    for neighbour in (up, below):
        pl.semaphore_signal(barrier, inc=1, device_id={"mp": neighbour}, device_id_type=MESH)
    for j in range(1, sections):
        other = lax.rem(sec + j, sections)
        pl.semaphore_signal(barrier, inc=1, device_id={"section": other}, device_id_type=MESH)

    def send(src, dst, send_sem, recv_sem, where):
        return pltpu.make_async_remote_copy(
            src_ref=src, dst_ref=dst, send_sem=send_sem, recv_sem=recv_sem,
            device_id=where, device_id_type=MESH,
        )

    def columns(way):
        return pl.ds(way * cut, cut)

    def product(r):
        loads[r].wait()
        acts = jnp.maximum(hidden[r], jnp.zeros((), hidden.dtype))
        made = jnp.dot(acts, down[...], preferred_element_type=jnp.float32)
        partial[r] = made.reshape(groups, GROUP, width)

    sums, passes, hops = {}, {}, {}
    neighbour_of = ({"mp": up}, {"mp": below})

    def start_sum(way, k, g):
        r = half - k if way == 0 else half + k
        src, dst = partial.at[r, g], arrived.at[way, k, g]
        if k == 0:
            src, dst = src.at[:, columns(way)], dst.at[:, columns(way)]
        copy = send(src, dst, sum_send.at[way, k, g], sum_recv.at[way, k, g], neighbour_of[way])
        copy.start()
        sums[way, k, g] = copy

    def start_pass(way, h, g):
        origin = lax.rem(me + (ring - (h - 1) if way == 0 else h - 1), ring)
        block = rows_all.at[origin, g]
        if h == half:
            block = block.at[:, columns(way)]
        copy = send(block, block, pass_send.at[way, h - 1, g], pass_recv.at[way, h - 1, g], neighbour_of[way])
        copy.start()
        passes[way, h, g] = copy

    loads["down"].wait()
    product(half)
    pl.semaphore_wait(barrier, 2 + sections - 1)
    for g in range(groups):
        for way in (0, 1):
            start_sum(way, 0, g)

    small = [send(gain_ref, next_gain, small_send.at[0], small_recv.at[0], {"section": before})]
    for j in range(1, sections):
        where = {"section": lax.rem(sec + j, sections)}
        small.append(send(counts.at[0], counts.at[j], small_send.at[j], small_recv.at[j], where))
    for copy in small:
        copy.start()

    for r in order[1:]:
        product(r)

    finish_ready = []

    def finish(g):
        for way in (0, 1):
            sums[way, half - 1, g].wait_recv()
        if not finish_ready:
            finish_ready.append(True)
            for copy in small:
                copy.wait_recv()
            loads["residual"].wait()
        depth = counts[0]
        for j in range(1, sections):
            depth = depth + counts[j]
        scale = 1.0 / jnp.sqrt(depth.astype(jnp.float32)[:1, :1])
        total = partial[0, g] + arrived[0, half - 1, g] + arrived[1, half - 1, g]
        span = pl.ds(g * GROUP, GROUP)
        stream = residual[span, :] + total * scale
        finished_ref[0, span, :] = stream
        mean_square = jnp.mean(stream * stream, axis=-1, keepdims=True)
        normed[g] = (stream * lax.rsqrt(mean_square + 1e-06) * next_gain[...]).astype(normed.dtype)
        copy = send(normed.at[g], rows_all.at[me, g], hop_send.at[g], hop_recv.at[g], {"section": after})
        copy.start()
        hops[g] = copy

    weights_ready = []

    def project(r):
        if not weights_ready:
            weights_ready.append(True)
            loads["qkv"].wait()
        origin = lax.rem(me + r, ring)
        block = rows_all[origin].astype(jnp.float32).reshape(rows, width).astype(rows_all.dtype)
        made = jnp.dot(block, qkv[...], preferred_element_type=jnp.float32)
        out_ref[origin] = made.astype(out_ref.dtype)

    for name, k, g in event_order(ring, groups):
        if name == "sum":
            for way in (0, 1):
                r = half - k if way == 0 else half + k
                sums[way, k - 1, g].wait_recv()
                if k == 1:
                    at = columns(way)
                    partial[r, g, :, at] = partial[r, g, :, at] + arrived[way, 0, g, :, at]
                else:
                    partial[r, g] = partial[r, g] + arrived[way, k - 1, g]
                start_sum(way, k, g)
        elif name == "finish":
            finish(g)
        else:
            if k == 1:
                hops[g].wait_recv()
                for way in (0, 1):
                    start_pass(way, 1, g)
            else:
                for way in (0, 1):
                    passes[way, k - 1, g].wait_recv()
                    start_pass(way, k, g)
            if g == groups - 1:
                if k == 1:
                    project(0)
                else:
                    project(ring - (k - 1))
                    project(k - 1)

    for g in range(groups):
        for way in (0, 1):
            passes[way, half, g].wait_recv()
    project(half)

    for copies in (small, sums.values(), hops.values(), passes.values()):
        for copy in copies:
            copy.wait_send()


def body(ring, sections, residual_in, pre_activation, down_projection, attention_gain, qkv_projection, layer_counts):
    rows, width = residual_in.shape[1:]
    hidden_units = down_projection.shape[1]
    qkv_matrix = qkv_projection[0].reshape(width, -1)
    out_width = qkv_matrix.shape[1]
    groups, half = rows // GROUP, ring // 2
    any_space = pl.BlockSpec(memory_space=pl.ANY)
    dma = pltpu.SemaphoreType.DMA
    finished, product = pl.pallas_call(
        functools.partial(kernel, ring, sections),
        out_shape=(
            jax.ShapeDtypeStruct(residual_in.shape, jnp.float32),
            jax.ShapeDtypeStruct((ring, rows, out_width), jnp.bfloat16),
        ),
        in_specs=[any_space] * 5 + [pl.BlockSpec(memory_space=pltpu.SMEM)],
        out_specs=(pl.BlockSpec(memory_space=pltpu.VMEM), pl.BlockSpec(memory_space=pltpu.VMEM)),
        scratch_shapes=[
            pltpu.VMEM((ring, rows, hidden_units), jnp.bfloat16),
            pltpu.VMEM((hidden_units, width), jnp.bfloat16),
            pltpu.VMEM((width, out_width), jnp.bfloat16),
            pltpu.VMEM((rows, width), jnp.float32),
            pltpu.VMEM((1, width), jnp.float32),
            pltpu.VMEM((sections, 8, 128), jnp.int32),
            pltpu.VMEM((ring, groups, GROUP, width), jnp.float32),
            pltpu.VMEM((2, half, groups, GROUP, width), jnp.float32),
            pltpu.VMEM((groups, GROUP, width), jnp.bfloat16),
            pltpu.VMEM((ring, groups, GROUP, width), jnp.bfloat16),
            dma((ring + 3,)),
            dma((sections,)),
            dma((sections,)),
            dma((2, half, groups)),
            dma((2, half, groups)),
            dma((groups,)),
            dma((groups,)),
            dma((2, half, groups)),
            dma((2, half, groups)),
        ],
        compiler_params=pltpu.CompilerParams(
            collective_id=0, has_side_effects=True, vmem_limit_bytes=32 * 1024 * 1024
        ),
    )(residual_in, pre_activation, down_projection, attention_gain, qkv_matrix, layer_counts)
    heads, head_width = qkv_projection.shape[2:]
    return finished, product.reshape(1, ring * rows, heads, head_width)


def solution(mesh):
    return jax.shard_map(
        functools.partial(body, mesh.shape["mp"], mesh.shape["section"]),
        mesh=mesh,
        in_specs=(
            P("section", ("dp", "mp"), None),
            P("section", "dp", "mp"),
            P("section", "mp", None),
            P("section", None),
            P("section", None, "mp", None),
            P("section"),
        ),
        out_specs=(P("section", ("dp", "mp"), None), P("section", "dp", "mp", None)),
        check_vma=False,
    )
```
